32 devices in a mesh: epoch: 4 (over y, x), sky: 8 (over z, core).
Axes of the slice: x: 2, y: 2, z: 4, core: 2. Of those that a mesh axis runs over, the one named last changes fastest.
Arguments:
- image: bfloat16 [16, 384, 2048], P('epoch', 'sky'), may hold values from -400 to 400
- inv_variance: bfloat16 [16, 384, 2048], P('epoch', 'sky'), may hold values from 0.25 to 4
- psf_rows: float32 [9], replicated, may hold values from 0.05 to 1
- psf_cols: float32 [9], replicated, may hold values from 0.05 to 1
- shift_num: int32 [4, 16], replicated, may hold values from -64 to 64, as said below
Outputs:
- search_map: float32 [384, 2048], P('sky', 'epoch')
The draws below stay inside these ranges and needn't reach their ends.
Inputs may be any that keep to these rules, and one draw needn't show every extreme that they name: `shift_num`: at level l every entry has magnitude at most 4 * 2 * 2^l, and at each level some entry equals plus and some other entry minus that bound.
All inputs are finite; a program needn't handle non-finite values.
Results may differ from the reference program's by a relative error of at most 0.0024.
Values may be sent and summed in bfloat16 or wider, within the bound.
A program may use at most 64 MiB of HBM per device.

```python
import math
import jax
import jax.numpy as jnp
from jax import lax

EPOCHS = 16
LEVELS = 4
COLS = 2048
PSF_HALF = 4
DEN = 4
VMAX = 2
ROWS = 384


def draw_image(key, part):
    key_base = jax.random.fold_in(jax.random.fold_in(key, 11), 0)
    base_values = jax.random.normal(key_base, (EPOCHS, ROWS, COLS), jnp.float32)
    return jnp.clip(base_values, -6.0, 6.0).astype(jnp.bfloat16)


def draw_shift_num(key, part):
    key_raw, key_top, key_low = jax.random.split(jax.random.fold_in(key, 23), 3)
    limits = DEN * VMAX * (2 ** jnp.arange(LEVELS, dtype=jnp.int32))[:, None]
    raw_values = jax.random.randint(key_raw, (LEVELS, EPOCHS), 0, 1 << 20, dtype=jnp.int32)
    values = raw_values % (2 * limits + 1) - limits
    column = jnp.arange(EPOCHS, dtype=jnp.int32)[None, :]
    top_pos = jax.random.randint(key_top, (LEVELS, 1), 0, EPOCHS, dtype=jnp.int32)
    low_pos = (top_pos + 1 + jax.random.randint(key_low, (LEVELS, 1), 0, EPOCHS - 1, dtype=jnp.int32)) % EPOCHS
    values = jnp.where(column == top_pos, limits, jnp.where(column == low_pos, -limits, values))
    return values.astype(jnp.int32)


def levels(stream_key, extent, cuts, least, top_value):
    def one(dim, blocks):
        steps = jax.random.uniform(jax.random.fold_in(jax.random.fold_in(stream_key, 6), dim), (blocks,), jnp.float32, least / len(cuts), top_value / len(cuts))
        return jnp.repeat(jnp.exp(steps), extent[dim] // blocks).reshape((-1,) + (1,) * (len(extent) - dim - 1))

    level = one(*cuts[0])
    for cut in cuts[1:]:
        level = level * one(*cut)
    return level


def setup_inputs(seed: int = 0) -> dict:
    arg_keys = jax.random.split(jax.random.key(seed), 6)
    return {
        "image": draw_image(jax.random.fold_in(arg_keys[5], 71), 0),
        "inv_variance": jnp.clip(jnp.exp(math.log(4.0) - 2.7725887 * jax.random.uniform(arg_keys[1], (EPOCHS, ROWS, COLS), jnp.float32) ** levels(arg_keys[1], (EPOCHS, ROWS, COLS), ((0, 4), (1, 8)), -0.2, 0.2)), 0.25, 4.0).astype(jnp.bfloat16),
        "psf_rows": jnp.clip(jnp.exp(jax.random.uniform(arg_keys[2], (2 * PSF_HALF + 1,), jnp.float32, math.log(0.05), math.log(1.0))), 0.05, 1.0),
        "psf_cols": jnp.clip(jnp.exp(jax.random.uniform(arg_keys[3], (2 * PSF_HALF + 1,), jnp.float32, math.log(0.05), math.log(1.0))), 0.05, 1.0),
        "shift_num": draw_shift_num(jax.random.fold_in(arg_keys[5], 71), 0),
    }


def filter_epoch(pixels, weights_in, psf_rows, psf_cols):
    reach = PSF_HALF
    weighted = pixels * weights_in
    weighted_pad = jnp.pad(weighted, ((reach, reach), (reach, reach)))
    variance_pad = jnp.pad(weights_in, ((reach, reach), (reach, reach)))
    row_count = pixels.shape[0]
    col_count = pixels.shape[1]
    rows_psi = jnp.zeros((row_count, col_count + 2 * reach), jnp.float32)
    rows_phi = jnp.zeros((row_count, col_count + 2 * reach), jnp.float32)
    for offset in range(2 * reach + 1):
        rows_psi = rows_psi + psf_rows[offset] * weighted_pad[offset:offset + row_count, :]
        rows_phi = rows_phi + psf_rows[offset] * psf_rows[offset] * variance_pad[offset:offset + row_count, :]
    psi_map = jnp.zeros((row_count, col_count), jnp.float32)
    phi_map = jnp.zeros((row_count, col_count), jnp.float32)
    for offset in range(2 * reach + 1):
        psi_map = psi_map + psf_cols[offset] * rows_psi[:, offset:offset + col_count]
        phi_map = phi_map + psf_cols[offset] * psf_cols[offset] * rows_phi[:, offset:offset + col_count]
    return jnp.stack([psi_map, phi_map])

def shift_rows(padded, numerators, rim_width):
    row_count = padded.shape[2] - 2 * rim_width
    whole_rows = jnp.floor_divide(numerators, DEN)
    fraction = (numerators - whole_rows * DEN).astype(jnp.float32) / DEN
    start_rows = (rim_width - whole_rows - 1).astype(jnp.int32)

    def take_rows(one_block, start):
        return lax.dynamic_slice_in_dim(one_block, start, row_count + 1, axis=1)
    taken_rows = jax.vmap(take_rows)(padded, start_rows)
    fraction = fraction[:, None, None, None]
    return (1.0 - fraction) * taken_rows[:, :, 1:] + fraction * taken_rows[:, :, :-1]

def reference(image, inv_variance, psf_rows, psf_cols, shift_num):

    def one_epoch(pair):
        return filter_epoch(pair[0].astype(jnp.float32), pair[1].astype(jnp.float32), psf_rows, psf_cols)
    stacks = lax.map(one_epoch, jnp.stack([image, inv_variance], axis=1))
    row_count = stacks.shape[2]
    col_count = stacks.shape[3]
    for level_index in range(LEVELS):
        half_span = 2 ** level_index
        groups = EPOCHS // (2 * half_span)
        rim_width = VMAX * half_span + 1
        paired = stacks.reshape(groups, 2, half_span, 2, row_count, col_count)
        lower_half = paired[:, 0].reshape(groups * half_span, 2, row_count, col_count)
        upper_half = paired[:, 1].reshape(groups * half_span, 2, row_count, col_count)
        numerators = shift_num[level_index].reshape(groups, 2, half_span)
        padded = jnp.pad(upper_half, ((0, 0), (0, 0), (rim_width, rim_width), (0, 0)))
        new_lower = lower_half + shift_rows(padded, numerators[:, 0].reshape(-1), rim_width)
        new_upper = lower_half + shift_rows(padded, numerators[:, 1].reshape(-1), rim_width)
        stacks = jnp.stack([new_lower.reshape(groups, half_span, 2, row_count, col_count), new_upper.reshape(groups, half_span, 2, row_count, col_count)], axis=1)
        stacks = stacks.reshape(EPOCHS, 2, row_count, col_count)
    likelihood = stacks[:, 0] / jnp.sqrt(stacks[:, 1])
    peak_value = lax.optimization_barrier(jnp.max(likelihood, axis=0))
    return peak_value + jnp.log(lax.optimization_barrier(jnp.sum(jnp.exp(likelihood - peak_value[None]), axis=0)))
```

```python
import functools

import jax
import jax.numpy as jnp
from jax import lax
from jax.experimental import pallas as pl
from jax.experimental.pallas import tpu as pltpu
from jax.sharding import PartitionSpec as P

LEVELS = 4
PSF_HALF = 4
DEN = 4
VMAX = 2
LANES = 128
SUB = 8
BSUB = 16
MESH = pl.DeviceIdType.MESH


def flip(index, mask, size):
    result, bit = 0, 1
    while bit < size:
        digit = lax.rem(lax.div(index, bit), 2)
        result = result + bit * ((1 - digit) if mask & bit else digit)
        bit *= 2
    return result


def up_to(value, step):
    return (value + step - 1) // step


def kernel(
    n, sky, image, variance, psf_rows, psf_cols, shift_num, out,
    outgoing, pieces, above, below, rows_in, *rest,
):
    sems = rest[-6:]
    send_sem, recv_sem, down_send, down_recv, up_send, up_recv = sems
    stacks = rest[:-6]
    ep_local, row_count = image.shape[0], image.shape[1]
    tiles = image.shape[2] // n // LANES
    width = tiles * LANES
    blocks = row_count // SUB
    reach = PSF_HALF
    local_levels = ep_local.bit_length() - 1
    me = lax.axis_index("epoch")
    row_dev = lax.axis_index("sky")
    has_above = row_dev > 0
    has_below = row_dev < sky - 1
    groups = [flip(me, d, n) for d in range(n)]

    barrier = pltpu.get_barrier_semaphore()
    for d in range(1, n):
        pl.semaphore_signal(barrier, inc=1, device_id=(groups[d], row_dev), device_id_type=MESH)

    @pl.when(has_above)
    def _():
        pl.semaphore_signal(barrier, inc=1, device_id=(me, row_dev - 1), device_id_type=MESH)

    @pl.when(has_below)
    def _():
        pl.semaphore_signal(barrier, inc=1, device_id=(me, row_dev + 1), device_id_type=MESH)

    lane = lax.broadcasted_iota(jnp.int32, (BSUB, LANES), 1)

    def filter_cols(p, dest):
        left_on = jnp.where(p > 0, 1.0, 0.0).astype(jnp.float32)
        right_on = jnp.where(p < n - 1, 1.0, 0.0).astype(jnp.float32)
        start = p * width
        starts = [jnp.maximum(start - LANES, 0)]
        starts += [start + c * LANES for c in range(tiles)]
        starts += [jnp.minimum(start + width, (n * tiles - 1) * LANES)]
        starts = [pl.multiple_of(at, LANES) for at in starts]
        w = [psf_cols[b] for b in range(2 * reach + 1)]

        def body(i, carry):
            e = lax.div(i, row_count // BSUB)
            r = pl.multiple_of(lax.rem(i, row_count // BSUB) * BSUB, BSUB)
            var, wgt = [], []
            for t, at in enumerate(starts):
                v = variance[e, pl.ds(r, BSUB), pl.ds(at, LANES)].astype(jnp.float32)
                if t == 0:
                    v = v * left_on
                if t == tiles + 1:
                    v = v * right_on
                x = image[e, pl.ds(r, BSUB), pl.ds(at, LANES)].astype(jnp.float32)
                var.append(v)
                wgt.append(x * v)
            for m, src in enumerate((wgt, var)):
                weights = w if m == 0 else [s * s for s in w]
                sums = [weights[reach] * src[c + 1] for c in range(tiles)]
                for b in range(2 * reach + 1):
                    off = b - reach
                    if off == 0:
                        continue
                    if off > 0:
                        turned = [pltpu.roll(x, LANES - off, 1) for x in src[1:]]
                        for c in range(tiles):
                            moved = jnp.where(lane < LANES - off, turned[c], turned[c + 1])
                            sums[c] = sums[c] + weights[b] * moved
                    else:
                        turned = [pltpu.roll(x, -off, 1) for x in src[:-1]]
                        for c in range(tiles):
                            moved = jnp.where(lane >= -off, turned[c + 1], turned[c])
                            sums[c] = sums[c] + weights[b] * moved
                for c in range(tiles):
                    dest[e, m, c, pl.ds(r, BSUB), :] = sums[c].astype(jnp.bfloat16)
            return carry

        lax.fori_loop(0, ep_local * (row_count // BSUB), body, 0)

    def piece_copy(d):
        return pltpu.make_async_remote_copy(
            src_ref=outgoing.at[d - 1], dst_ref=pieces.at[d],
            send_sem=send_sem.at[d], recv_sem=recv_sem.at[d],
            device_id=(groups[d], row_dev), device_id_type=MESH,
        )

    def halo_rows(g):
        last = (g + 1) * ep_local - 1
        return BSUB * up_to(SUB * up_to(VMAX * last, SUB) + reach, BSUB)

    def to_below(d, g):
        h = halo_rows(g)
        rows = pl.ds(row_count - h, h)
        return pltpu.make_async_remote_copy(
            src_ref=pieces.at[d, :, :, :, rows, :], dst_ref=above.at[d, :, :, :, rows, :],
            send_sem=down_send.at[d], recv_sem=down_recv.at[d],
            device_id=(me, row_dev + 1), device_id_type=MESH,
        )

    def to_above(d, g):
        rows = pl.ds(0, halo_rows(g))
        return pltpu.make_async_remote_copy(
            src_ref=pieces.at[d, :, :, :, rows, :], dst_ref=below.at[d, :, :, :, rows, :],
            send_sem=up_send.at[d], recv_sem=up_recv.at[d],
            device_id=(me, row_dev - 1), device_id_type=MESH,
        )

    def each_group(d, use):
        for g in range(n):
            pl.when(groups[d] == g)(functools.partial(use, g))

    def forward(d):
        def use(g):
            @pl.when(has_below)
            def _():
                to_below(d, g).start()

            @pl.when(has_above)
            def _():
                to_above(d, g).start()

        each_group(d, use)

    def wait_halo(d):
        def use(g):
            @pl.when(has_above)
            def _():
                to_below(d, g).wait_recv()

            @pl.when(has_below)
            def _():
                to_above(d, g).wait_recv()

        each_group(d, use)

    def wait_sent(d):
        def use(g):
            @pl.when(has_below)
            def _():
                to_below(d, g).wait_send()

            @pl.when(has_above)
            def _():
                to_above(d, g).wait_send()

        each_group(d, use)

    def bounds(pad):
        low = jnp.where(has_above, -pad, 0)
        high = jnp.where(has_below, blocks + pad, blocks)
        return low, high

    def row_at(block):
        return pl.multiple_of(row_count + block * SUB, SUB)

    slabs = [(m, c) for m in range(2) for c in range(tiles)]

    def unpack(d, g):
        last = (g + 1) * ep_local - 1
        count = up_to(SUB * up_to(VMAX * last, SUB) + reach, BSUB)
        per = row_count // BSUB

        def rows_of(source, part, low, high):
            def body(i, carry):
                r = pl.multiple_of(i * BSUB, BSUB)
                to = pl.multiple_of(part * row_count + i * BSUB, BSUB)
                for e in range(ep_local):
                    for m, c in slabs:
                        rows_in[e, m, c, pl.ds(to, BSUB), :] = source[
                            d, e, m, c, pl.ds(r, BSUB), :
                        ].astype(jnp.float32)
                return carry

            lax.fori_loop(low, high, body, 0)

        rows_of(above, 0, jnp.where(has_above, per - count, per), per)
        rows_of(pieces, 1, 0, per)
        rows_of(below, 2, 0, jnp.where(has_below, count, 0))

    def filter_rows(g, dest):
        w = [psf_rows[b] for b in range(2 * reach + 1)]
        squares = [s * s for s in w]

        def one_epoch(e, carry):
            low, high = bounds(up_to(VMAX * (g * ep_local + e), SUB))

            def body(b, carry):
                at = row_at(b)
                for m, c in slabs:
                    weights = w if m == 0 else squares
                    total = weights[reach] * rows_in[e, m, c, pl.ds(at, SUB), :]
                    for a in range(2 * reach + 1):
                        if a != reach:
                            total = total + weights[a] * rows_in[
                                e, m, c, pl.ds(at + (a - reach), SUB), :
                            ]
                    dest[e, m, c, pl.ds(at, SUB), :] = total
                return carry

            return lax.fori_loop(low, high, body, carry)

        lax.fori_loop(0, ep_local, one_epoch, 0)

    def shift_of(level, index):
        number = shift_num[level, index]
        big = 2 * VMAX * 2**LEVELS
        whole = lax.div(number + DEN * big, DEN) - big
        left = number - whole * DEN
        fraction = left.astype(jnp.float32) / DEN
        return whole, whole + jnp.where(left > 0, 1, 0), fraction

    def level_pass(level, src, dest, base, count, dest_base):
        half = 2**level

        def one_pair(pair, carry):
            j = lax.div(pair, half) * (2 * half) + lax.rem(pair, half)
            k = j + half
            first = base + lax.div(pair, half) * (2 * half)
            low, high = bounds(up_to(VMAX * first, SUB))
            moves = [(j, shift_of(level, base + j)), (k, shift_of(level, base + k))]

            def body(b, carry):
                at = row_at(b)
                for m, c in slabs:
                    lower = src[j, m, c, pl.ds(at, SUB), :]
                    for index, (near, far, fraction) in moves:
                        x = src[k, m, c, pl.ds(at - near, SUB), :]
                        y = src[k, m, c, pl.ds(at - far, SUB), :]
                        dest[dest_base + index, m, c, pl.ds(at, SUB), :] = lower + (
                            (1.0 - fraction) * x + fraction * y
                        )
                return carry

            return lax.fori_loop(low, high, body, carry)

        lax.fori_loop(0, count // 2, one_pair, 0)

    local, wide = stacks[:local_levels], stacks[local_levels:]

    def process(d):
        g = groups[d]
        wait_halo(d)
        unpack(d, g)
        filter_rows(g, local[0])
        for level in range(local_levels):
            last = level == local_levels - 1
            level_pass(
                level, local[level], wide[0] if last else local[level + 1],
                g * ep_local, ep_local, g * ep_local if last else 0,
            )

    order = [n - 1] + list(range(1, n - 1))
    waited = False
    for d in order + [0]:
        filter_cols(groups[d], outgoing.at[d - 1] if d else pieces.at[0])
        if not waited:
            near = jnp.where(has_above, 1, 0) + jnp.where(has_below, 1, 0)
            pl.semaphore_wait(barrier, n - 1 + near)
            waited = True
        if d:
            piece_copy(d).start()
        else:
            forward(0)

    for edge, part in ((has_above, 0), (has_below, 2)):
        @pl.when(jnp.logical_not(edge))
        def _():
            for ref in (rows_in,) + stacks:
                zero = jnp.zeros((row_count, LANES), jnp.float32)

                def body(e, carry):
                    for m, c in slabs:
                        ref[e, m, c, pl.ds(part * row_count, row_count), :] = zero
                    return carry

                lax.fori_loop(0, ref.shape[0], body, 0)

    for d in range(1, n):
        piece_copy(d).wait_recv()
        forward(d)
        process(d - 1)
    process(n - 1)

    epochs = n * ep_local
    for level in range(local_levels, LEVELS - 1):
        level_pass(
            level, wide[level - local_levels], wide[level - local_levels + 1], 0, epochs, 0
        )

    final = wide[LEVELS - 1 - local_levels]
    half = epochs // 2

    def finish(b, carry):
        at = row_at(b)
        for c in range(tiles):
            likelihood = [None] * epochs
            for j in range(half):
                lower = [final[j, m, c, pl.ds(at, SUB), :] for m in range(2)]
                for index in (j, j + half):
                    near, far, fraction = shift_of(LEVELS - 1, index)
                    maps = []
                    for m in range(2):
                        x = final[j + half, m, c, pl.ds(at - near, SUB), :]
                        y = final[j + half, m, c, pl.ds(at - far, SUB), :]
                        maps.append(lower[m] + ((1.0 - fraction) * x + fraction * y))
                    likelihood[index] = maps[0] * lax.rsqrt(maps[1])
            peak = functools.reduce(jnp.maximum, likelihood)
            total = functools.reduce(jnp.add, [jnp.exp(x - peak) for x in likelihood])
            to = pl.multiple_of(b * SUB, SUB)
            out[pl.ds(to, SUB), c * LANES:(c + 1) * LANES] = peak + jnp.log(total)
        return carry

    lax.fori_loop(0, blocks, finish, 0)

    for d in range(1, n):
        piece_copy(d).wait_send()
    for d in range(n):
        wait_sent(d)


def on_device(n, sky, image, inv_variance, psf_rows, psf_cols, shift_num):
    ep_local, row_count, cols = image.shape
    tiles = cols // n // LANES
    epochs = n * ep_local
    local_levels = ep_local.bit_length() - 1
    piece = (ep_local, 2, tiles, row_count, LANES)

    def tall(count):
        return pltpu.VMEM((count, 2, tiles, 3 * row_count, LANES), jnp.float32)

    vmem = pl.BlockSpec(memory_space=pltpu.VMEM)
    smem = pl.BlockSpec(memory_space=pltpu.SMEM)
    return pl.pallas_call(
        functools.partial(kernel, n, sky),
        out_shape=jax.ShapeDtypeStruct((row_count, cols // n), jnp.float32),
        in_specs=[vmem, vmem, smem, smem, smem],
        out_specs=vmem,
        scratch_shapes=[
            pltpu.VMEM((n - 1,) + piece, jnp.bfloat16),
            pltpu.VMEM((n,) + piece, jnp.bfloat16),
            pltpu.VMEM((n,) + piece, jnp.bfloat16),
            pltpu.VMEM((n,) + piece, jnp.bfloat16),
            tall(ep_local),
        ]
        + [tall(ep_local) for _ in range(local_levels)]
        + [tall(epochs) for _ in range(LEVELS - local_levels)]
        + [pltpu.SemaphoreType.DMA((n,)) for _ in range(6)],
        compiler_params=pltpu.CompilerParams(
            collective_id=0, has_side_effects=True, vmem_limit_bytes=60 * 1024 * 1024
        ),
    )(image, inv_variance, psf_rows, psf_cols, shift_num)


def solution(mesh):
    body = functools.partial(on_device, mesh.shape["epoch"], mesh.shape["sky"])
    return jax.shard_map(
        body,
        mesh=mesh,
        in_specs=(P("epoch", "sky", None), P("epoch", "sky", None), P(), P(), P()),
        out_specs=P("sky", "epoch"),
        check_vma=False,
    )
```

```python
import functools

import jax
import jax.numpy as jnp
from jax import lax
from jax.experimental import pallas as pl
from jax.experimental.pallas import tpu as pltpu
from jax.sharding import PartitionSpec as P

LEVELS = 4
PSF_HALF = 4
DEN = 4
VMAX = 2
LANES = 128
SUB = 8
BSUB = 16
MESH = pl.DeviceIdType.MESH


def flip(index, mask, size):
    result, bit = 0, 1
    while bit < size:
        digit = lax.rem(lax.div(index, bit), 2)
        result = result + bit * ((1 - digit) if mask & bit else digit)
        bit *= 2
    return result


def up_to(value, step):
    return (value + step - 1) // step


LAG = 3


def SEND_ORDER(n):
    return list(range(1, n)) + [0]


def kernel(
    n, sky, image, variance, psf_rows, psf_cols, shift_num, out,
    outgoing, pieces, above, below, bands, rows_in, *rest,
):
    send_sem, recv_sem, down_send, down_recv, up_send, up_recv = rest[-6:]
    stacks = rest[:-6]
    ep_local, row_count = image.shape[0], image.shape[1]
    epochs = n * ep_local
    tiles = image.shape[2] // n // LANES
    blocks = row_count // SUB
    reach = PSF_HALF
    local_levels = ep_local.bit_length() - 1
    me = lax.axis_index("epoch")
    row_dev = lax.axis_index("sky")
    has_above = row_dev > 0
    has_below = row_dev < sky - 1
    groups = [flip(me, d, n) for d in range(n)]

    barrier = pltpu.get_barrier_semaphore()
    for d in range(1, n):
        pl.semaphore_signal(barrier, inc=1, device_id=(groups[d], row_dev), device_id_type=MESH)

    @pl.when(has_above)
    def _():
        pl.semaphore_signal(barrier, inc=1, device_id=(me, row_dev - 1), device_id_type=MESH)

    @pl.when(has_below)
    def _():
        pl.semaphore_signal(barrier, inc=1, device_id=(me, row_dev + 1), device_id_type=MESH)

    def make_bands():
        source = lax.broadcasted_iota(jnp.int32, (2 * LANES, LANES), 0)
        column = lax.broadcasted_iota(jnp.int32, (2 * LANES, LANES), 1)
        at = jnp.where(source < LANES + LANES // 2, source, source - 2 * LANES)
        tap = at - column + reach
        for m in range(2):
            band = jnp.zeros((2 * LANES, LANES), jnp.float32)
            for b in range(2 * reach + 1):
                weight = psf_cols[b] if m == 0 else psf_cols[b] * psf_cols[b]
                band = jnp.where(tap == b, weight, band)
            high = band.astype(jnp.bfloat16)
            bands[m, :, :LANES] = high
            bands[m, :, LANES:] = (band - high.astype(jnp.float32)).astype(jnp.bfloat16)

    lane = lax.broadcasted_iota(jnp.int32, (ep_local * row_count, LANES), 1)

    def filter_cols(p, tile, dest):
        here = p * tiles + tile
        flat = (ep_local * row_count, LANES)

        def take(ref, t):
            at = pl.multiple_of(t * LANES, LANES)
            return ref[:, :, pl.ds(at, LANES)].astype(jnp.float32).reshape(flat)

        def both(t, keep):
            v = take(variance, t)
            if keep is not None:
                v = v * keep
            return take(image, t) * v, v

        total = n * tiles
        left_on = jnp.where(here > 0, 1.0, 0.0).astype(jnp.float32)
        right_on = jnp.where(here < total - 1, 1.0, 0.0).astype(jnp.float32)
        left = both(jnp.maximum(here - 1, 0), left_on)
        centre = both(here, None)
        right = both(jnp.minimum(here + 1, total - 1), right_on)
        for m in range(2):
            edge = jnp.where(lane < LANES // 2, right[m], left[m])
            x = jnp.concatenate([centre[m], edge], axis=1)
            high = x.astype(jnp.bfloat16)
            y = jnp.dot(high, bands[m], preferred_element_type=jnp.float32)
            y = y[:, :LANES] + y[:, LANES:]
            if m == 0:
                low = (x - high.astype(jnp.float32)).astype(jnp.bfloat16)
                y = y + jnp.dot(low, bands[m, :, :LANES], preferred_element_type=jnp.float32)
            dest[:, m] = y.reshape(ep_local, row_count, LANES).astype(jnp.bfloat16)

    def piece_copy(d, tile):
        return pltpu.make_async_remote_copy(
            src_ref=outgoing.at[d - 1, tile], dst_ref=pieces.at[d, tile],
            send_sem=send_sem.at[d, tile], recv_sem=recv_sem.at[d, tile],
            device_id=(groups[d], row_dev), device_id_type=MESH,
        )

    def halo_rows(g):
        last = (g + 1) * ep_local - 1
        return BSUB * up_to(SUB * up_to(VMAX * last, SUB) + reach, BSUB)

    def to_below(d, tile, g):
        h = halo_rows(g)
        rows = pl.ds(row_count - h, h)
        return pltpu.make_async_remote_copy(
            src_ref=pieces.at[d, tile, :, :, rows, :], dst_ref=above.at[d, tile, :, :, rows, :],
            send_sem=down_send.at[d, tile], recv_sem=down_recv.at[d, tile],
            device_id=(me, row_dev + 1), device_id_type=MESH,
        )

    def to_above(d, tile, g):
        rows = pl.ds(0, halo_rows(g))
        return pltpu.make_async_remote_copy(
            src_ref=pieces.at[d, tile, :, :, rows, :], dst_ref=below.at[d, tile, :, :, rows, :],
            send_sem=up_send.at[d, tile], recv_sem=up_recv.at[d, tile],
            device_id=(me, row_dev - 1), device_id_type=MESH,
        )

    def each_group(d, use):
        for g in range(n):
            pl.when(groups[d] == g)(functools.partial(use, g))

    def forward(d, tile):
        def use(g):
            @pl.when(has_below)
            def _():
                to_below(d, tile, g).start()

            @pl.when(has_above)
            def _():
                to_above(d, tile, g).start()

        each_group(d, use)

    def wait_halo(d, tile):
        def use(g):
            @pl.when(has_above)
            def _():
                to_below(d, tile, g).wait_recv()

            @pl.when(has_below)
            def _():
                to_above(d, tile, g).wait_recv()

        each_group(d, use)

    def wait_sent(d, tile):
        def use(g):
            @pl.when(has_below)
            def _():
                to_below(d, tile, g).wait_send()

            @pl.when(has_above)
            def _():
                to_above(d, tile, g).wait_send()

        each_group(d, use)

    def bounds(pad):
        low = jnp.where(has_above, -pad, 0)
        high = jnp.where(has_below, blocks + pad, blocks)
        return low, high

    def row_at(block):
        return pl.multiple_of(row_count + block * SUB, SUB)

    def unpack(d, tile, g):
        last = (g + 1) * ep_local - 1
        count = up_to(SUB * up_to(VMAX * last, SUB) + reach, BSUB)
        per = row_count // BSUB

        def rows_of(source, part, low, high):
            def body(i, carry):
                r = pl.multiple_of(i * BSUB, BSUB)
                to = pl.multiple_of(part * row_count + i * BSUB, BSUB)
                for e in range(ep_local):
                    for m in range(2):
                        rows_in[e, m, pl.ds(to, BSUB), :] = source[
                            d, tile, e, m, pl.ds(r, BSUB), :
                        ].astype(jnp.float32)
                return carry

            lax.fori_loop(low, high, body, 0)

        rows_of(above, 0, jnp.where(has_above, per - count, per), per)
        rows_of(pieces, 1, 0, per)
        rows_of(below, 2, 0, jnp.where(has_below, count, 0))

    def filter_rows(g, dest):
        w = [psf_rows[b] for b in range(2 * reach + 1)]
        squares = [s * s for s in w]
        low, high = bounds(up_to(VMAX * ((g + 1) * ep_local - 1), SUB))

        def body(b, carry):
            at = row_at(b)
            for e in range(ep_local):
                for m in range(2):
                    weights = w if m == 0 else squares
                    total = weights[reach] * rows_in[e, m, pl.ds(at, SUB), :]
                    for a in range(2 * reach + 1):
                        if a != reach:
                            total = total + weights[a] * rows_in[
                                e, m, pl.ds(at + (a - reach), SUB), :
                            ]
                    dest[e, m, pl.ds(at, SUB), :] = total
            return carry

        lax.fori_loop(low, high, body, 0)

    def shift_of(level, index):
        number = shift_num[level, index]
        big = 2 * VMAX * 2**LEVELS
        whole = lax.div(number + DEN * big, DEN) - big
        left = number - whole * DEN
        fraction = left.astype(jnp.float32) / DEN
        return whole, whole + jnp.where(left > 0, 1, 0), fraction

    def level_pass(level, src, dest, base, pairs, pad, dest_base):
        half = 2**level
        moves = [
            (j, [(i, shift_of(level, base + i)) for i in (j, j + half)]) for j in pairs
        ]
        low, high = bounds(pad)

        def body(b, carry):
            at = row_at(b)
            for j, outs in moves:
                for m in range(2):
                    lower = src[j, m, pl.ds(at, SUB), :]
                    for index, (near, far, fraction) in outs:
                        x = src[j + half, m, pl.ds(at - near, SUB), :]
                        y = src[j + half, m, pl.ds(at - far, SUB), :]
                        dest[dest_base + index, m, pl.ds(at, SUB), :] = lower + (
                            (1.0 - fraction) * x + fraction * y
                        )
            return carry

        lax.fori_loop(low, high, body, 0)

    local, wide = stacks[:local_levels], stacks[local_levels:]

    def process(d, tile):
        g = groups[d]
        wait_halo(d, tile)
        unpack(d, tile, g)
        filter_rows(g, local[0])
        for level in range(local_levels):
            last = level == local_levels - 1
            half = 2**level
            pairs = [j for j in range(ep_local) if not j & half]
            top = g * ep_local + ep_local - 2 * half
            level_pass(
                level, local[level], wide[0] if last else local[level + 1],
                g * ep_local, pairs, up_to(VMAX * top, SUB), g * ep_local if last else 0,
            )

    def finish(tile):
        for level in range(local_levels, LEVELS - 1):
            half = 2**level
            for first in range(0, epochs, 2 * half):
                level_pass(
                    level, wide[level - local_levels], wide[level - local_levels + 1], 0,
                    list(range(first, first + half)), up_to(VMAX * first, SUB), 0,
                )
        final = wide[LEVELS - 1 - local_levels]
        half = epochs // 2

        def body(b, carry):
            at = row_at(b)
            likelihood = [None] * epochs
            for j in range(half):
                lower = [final[j, m, pl.ds(at, SUB), :] for m in range(2)]
                for index in (j, j + half):
                    near, far, fraction = shift_of(LEVELS - 1, index)
                    maps = []
                    for m in range(2):
                        x = final[j + half, m, pl.ds(at - near, SUB), :]
                        y = final[j + half, m, pl.ds(at - far, SUB), :]
                        maps.append(lower[m] + ((1.0 - fraction) * x + fraction * y))
                    likelihood[index] = maps[0] * lax.rsqrt(maps[1])
            peak = functools.reduce(jnp.maximum, likelihood)
            total = functools.reduce(jnp.add, [jnp.exp(x - peak) for x in likelihood])
            to = pl.multiple_of(b * SUB, SUB)
            out[pl.ds(to, SUB), tile * LANES:(tile + 1) * LANES] = peak + jnp.log(total)
            return carry

        lax.fori_loop(0, blocks, body, 0)

    make_bands()
    for tile in range(tiles):
        for d in SEND_ORDER(n):
            filter_cols(groups[d], tile, outgoing.at[d - 1, tile] if d else pieces.at[0, tile])
            if tile == 0 and d == SEND_ORDER(n)[0]:
                near = jnp.where(has_above, 1, 0) + jnp.where(has_below, 1, 0)
                pl.semaphore_wait(barrier, n - 1 + near)
            if d:
                piece_copy(d, tile).start()
            else:
                forward(0, tile)

    for edge, part in ((has_above, 0), (has_below, 2)):
        @pl.when(jnp.logical_not(edge))
        def _():
            for ref in (rows_in,) + stacks:
                zero = jnp.zeros((row_count, LANES), jnp.float32)

                def body(e, carry):
                    for m in range(2):
                        ref[e, m, pl.ds(part * row_count, row_count), :] = zero
                    return carry

                lax.fori_loop(0, ref.shape[0], body, 0)

    steps = [(tile, d) for tile in range(tiles) for d in range(n)]
    for i in range(len(steps) + LAG):
        if i < len(steps):
            tile, d = steps[i]
            if d:
                piece_copy(d, tile).wait_recv()
                forward(d, tile)
        if i >= LAG:
            tile, d = steps[i - LAG]
            process(d, tile)
            if d == n - 1:
                finish(tile)

    for tile, d in steps:
        if d:
            piece_copy(d, tile).wait_send()
        wait_sent(d, tile)


def on_device(n, sky, image, inv_variance, psf_rows, psf_cols, shift_num):
    ep_local, row_count, cols = image.shape
    tiles = cols // n // LANES
    local_levels = ep_local.bit_length() - 1
    piece = (tiles, ep_local, 2, row_count, LANES)

    def tall(count):
        return pltpu.VMEM((count, 2, 3 * row_count, LANES), jnp.float32)

    vmem = pl.BlockSpec(memory_space=pltpu.VMEM)
    smem = pl.BlockSpec(memory_space=pltpu.SMEM)
    return pl.pallas_call(
        functools.partial(kernel, n, sky),
        out_shape=jax.ShapeDtypeStruct((row_count, cols // n), jnp.float32),
        in_specs=[vmem, vmem, smem, smem, smem],
        out_specs=vmem,
        scratch_shapes=[
            pltpu.VMEM((n - 1,) + piece, jnp.bfloat16),
            pltpu.VMEM((n,) + piece, jnp.bfloat16),
            pltpu.VMEM((n,) + piece, jnp.bfloat16),
            pltpu.VMEM((n,) + piece, jnp.bfloat16),
            pltpu.VMEM((2, 2 * LANES, 2 * LANES), jnp.bfloat16),
            tall(ep_local),
        ]
        + [tall(ep_local) for _ in range(local_levels)]
        + [tall(n * ep_local) for _ in range(LEVELS - local_levels)]
        + [pltpu.SemaphoreType.DMA((n, tiles)) for _ in range(6)],
        compiler_params=pltpu.CompilerParams(
            collective_id=0, has_side_effects=True, vmem_limit_bytes=60 * 1024 * 1024
        ),
    )(image, inv_variance, psf_rows, psf_cols, shift_num)


def solution(mesh):
    body = functools.partial(on_device, mesh.shape["epoch"], mesh.shape["sky"])
    return jax.shard_map(
        body,
        mesh=mesh,
        in_specs=(P("epoch", "sky", None), P("epoch", "sky", None), P(), P(), P()),
        out_specs=P("sky", "epoch"),
        check_vma=False,
    )
```

```python
import functools

import jax
import jax.numpy as jnp
from jax import lax
from jax.experimental import pallas as pl
from jax.experimental.pallas import tpu as pltpu
from jax.sharding import PartitionSpec as P

LEVELS = 4
PSF_HALF = 4
DEN = 4
VMAX = 2
LANES = 128
SUB = 8
BSUB = 16
MESH = pl.DeviceIdType.MESH


def flip(index, mask, size):
    result, bit = 0, 1
    while bit < size:
        digit = lax.rem(lax.div(index, bit), 2)
        result = result + bit * ((1 - digit) if mask & bit else digit)
        bit *= 2
    return result


def up_to(value, step):
    return (value + step - 1) // step


LAG = 3
PAIRS = 2
STEP = 16


def SEND_ORDER(n):
    return list(range(1, n)) + [0]


def kernel(
    n, sky, image, variance, psf_rows, psf_cols, shift_num, out,
    outgoing, pieces, above, below, bands, rows_in, *rest,
):
    send_sem, recv_sem, down_send, down_recv, up_send, up_recv = rest[-6:]
    stacks = rest[:-6]
    ep_local, row_count = image.shape[0], image.shape[1]
    epochs = n * ep_local
    tiles = image.shape[2] // n // LANES
    blocks = row_count // SUB
    reach = PSF_HALF
    local_levels = ep_local.bit_length() - 1
    me = lax.axis_index("epoch")
    row_dev = lax.axis_index("sky")
    has_above = row_dev > 0
    has_below = row_dev < sky - 1
    groups = [flip(me, d, n) for d in range(n)]

    barrier = pltpu.get_barrier_semaphore()
    for d in range(1, n):
        pl.semaphore_signal(barrier, inc=1, device_id=(groups[d], row_dev), device_id_type=MESH)

    @pl.when(has_above)
    def _():
        pl.semaphore_signal(barrier, inc=1, device_id=(me, row_dev - 1), device_id_type=MESH)

    @pl.when(has_below)
    def _():
        pl.semaphore_signal(barrier, inc=1, device_id=(me, row_dev + 1), device_id_type=MESH)

    def make_bands():
        source = lax.broadcasted_iota(jnp.int32, (2 * LANES, LANES), 0)
        column = lax.broadcasted_iota(jnp.int32, (2 * LANES, LANES), 1)
        at = jnp.where(source < LANES + LANES // 2, source, source - 2 * LANES)
        tap = at - column + reach
        for m in range(2):
            band = jnp.zeros((2 * LANES, LANES), jnp.float32)
            for b in range(2 * reach + 1):
                weight = psf_cols[b] if m == 0 else psf_cols[b] * psf_cols[b]
                band = jnp.where(tap == b, weight, band)
            high = band.astype(jnp.bfloat16)
            bands[m, :, :LANES] = high
            bands[m, :, LANES:] = (band - high.astype(jnp.float32)).astype(jnp.bfloat16)

    lane = lax.broadcasted_iota(jnp.int32, (ep_local * row_count, LANES), 1)

    def filter_cols(p, tile, dest):
        here = p * tiles + tile
        flat = (ep_local * row_count, LANES)

        def take(ref, t):
            at = pl.multiple_of(t * LANES, LANES)
            return ref[:, :, pl.ds(at, LANES)].astype(jnp.float32).reshape(flat)

        def both(t, keep):
            v = take(variance, t)
            if keep is not None:
                v = v * keep
            return take(image, t) * v, v

        total = n * tiles
        left_on = jnp.where(here > 0, 1.0, 0.0).astype(jnp.float32)
        right_on = jnp.where(here < total - 1, 1.0, 0.0).astype(jnp.float32)
        left = both(jnp.maximum(here - 1, 0), left_on)
        centre = both(here, None)
        right = both(jnp.minimum(here + 1, total - 1), right_on)
        for m in range(2):
            edge = jnp.where(lane < LANES // 2, right[m], left[m])
            x = jnp.concatenate([centre[m], edge], axis=1)
            high = x.astype(jnp.bfloat16)
            y = jnp.dot(high, bands[m], preferred_element_type=jnp.float32)
            y = y[:, :LANES] + y[:, LANES:]
            if m == 0:
                low = (x - high.astype(jnp.float32)).astype(jnp.bfloat16)
                y = y + jnp.dot(low, bands[m, :, :LANES], preferred_element_type=jnp.float32)
            dest[:, m] = y.reshape(ep_local, row_count, LANES).astype(jnp.bfloat16)

    def piece_copy(d, tile):
        return pltpu.make_async_remote_copy(
            src_ref=outgoing.at[d - 1, tile], dst_ref=pieces.at[d, tile],
            send_sem=send_sem.at[d, tile], recv_sem=recv_sem.at[d, tile],
            device_id=(groups[d], row_dev), device_id_type=MESH,
        )

    def halo_rows(g):
        last = (g + 1) * ep_local - 1
        return BSUB * up_to(SUB * up_to(VMAX * last, SUB) + reach, BSUB)

    def to_below(d, tile, g):
        h = halo_rows(g)
        rows = pl.ds(row_count - h, h)
        return pltpu.make_async_remote_copy(
            src_ref=pieces.at[d, tile, :, :, rows, :], dst_ref=above.at[d, tile, :, :, rows, :],
            send_sem=down_send.at[d, tile], recv_sem=down_recv.at[d, tile],
            device_id=(me, row_dev + 1), device_id_type=MESH,
        )

    def to_above(d, tile, g):
        rows = pl.ds(0, halo_rows(g))
        return pltpu.make_async_remote_copy(
            src_ref=pieces.at[d, tile, :, :, rows, :], dst_ref=below.at[d, tile, :, :, rows, :],
            send_sem=up_send.at[d, tile], recv_sem=up_recv.at[d, tile],
            device_id=(me, row_dev - 1), device_id_type=MESH,
        )

    def each_group(d, use):
        for g in range(n):
            pl.when(groups[d] == g)(functools.partial(use, g))

    def forward(d, tile):
        def use(g):
            @pl.when(has_below)
            def _():
                to_below(d, tile, g).start()

            @pl.when(has_above)
            def _():
                to_above(d, tile, g).start()

        each_group(d, use)

    def wait_halo(d, tile):
        def use(g):
            @pl.when(has_above)
            def _():
                to_below(d, tile, g).wait_recv()

            @pl.when(has_below)
            def _():
                to_above(d, tile, g).wait_recv()

        each_group(d, use)

    def wait_sent(d, tile):
        def use(g):
            @pl.when(has_below)
            def _():
                to_below(d, tile, g).wait_send()

            @pl.when(has_above)
            def _():
                to_above(d, tile, g).wait_send()

        each_group(d, use)

    def bounds(pad):
        low = jnp.where(has_above, -pad, 0)
        high = jnp.where(has_below, row_count // STEP + pad, row_count // STEP)
        return low, high

    def row_at(block, step=STEP):
        return pl.multiple_of(row_count + block * step, step)

    def unpack(d, tile, g):
        last = (g + 1) * ep_local - 1
        count = up_to(SUB * up_to(VMAX * last, SUB) + reach, BSUB)
        per = row_count // BSUB

        def rows_of(source, part, low, high):
            def body(i, carry):
                r = pl.multiple_of(i * BSUB, BSUB)
                to = pl.multiple_of(part * row_count + i * BSUB, BSUB)
                for e in range(ep_local):
                    for m in range(2):
                        rows_in[e, m, pl.ds(to, BSUB), :] = source[
                            d, tile, e, m, pl.ds(r, BSUB), :
                        ].astype(jnp.float32)
                return carry

            lax.fori_loop(low, high, body, 0)

        rows_of(above, 0, jnp.where(has_above, per - count, per), per)
        rows_of(pieces, 1, 0, per)
        rows_of(below, 2, 0, jnp.where(has_below, count, 0))

    def filter_rows(g, dest):
        w = [psf_rows[b] for b in range(2 * reach + 1)]
        squares = [s * s for s in w]
        low, high = bounds(up_to(VMAX * ((g + 1) * ep_local - 1), STEP))

        def body(b, carry):
            at = row_at(b)
            totals = {}
            for e in range(ep_local):
                for m in range(2):
                    weights = w if m == 0 else squares
                    parts = [
                        weights[a] * rows_in[e, m, pl.ds(at + (a - reach), STEP), :]
                        for a in range(2 * reach + 1)
                    ]
                    totals[e, m] = functools.reduce(jnp.add, parts)
            for (e, m), total in totals.items():
                dest[e, m, pl.ds(at, STEP), :] = total
            return carry

        lax.fori_loop(low, high, body, 0)

    def shift_of(level, index):
        number = shift_num[level, index]
        big = 2 * VMAX * 2**LEVELS
        whole = lax.div(number + DEN * big, DEN) - big
        left = number - whole * DEN
        fraction = left.astype(jnp.float32) / DEN
        return whole, whole + jnp.where(left > 0, 1, 0), fraction

    def level_pass(level, src, dest, base, pairs, pad, dest_base):
        half = 2**level
        moves = [
            (j, [(i, shift_of(level, base + i)) for i in (j, j + half)]) for j in pairs
        ]
        low, high = bounds(pad)

        def body(b, carry):
            at = row_at(b)
            for some in range(0, len(moves), PAIRS):
                results = []
                for j, outs in moves[some:some + PAIRS]:
                    for m in range(2):
                        lower = src[j, m, pl.ds(at, STEP), :]
                        for index, (near, far, fraction) in outs:
                            x = src[j + half, m, pl.ds(at - near, STEP), :]
                            y = src[j + half, m, pl.ds(at - far, STEP), :]
                            mixed = (1.0 - fraction) * x + fraction * y
                            results.append((index, m, lower + mixed))
                for index, m, result in results:
                    dest[dest_base + index, m, pl.ds(at, STEP), :] = result
            return carry

        lax.fori_loop(low, high, body, 0)

    local, wide = stacks[:local_levels], stacks[local_levels:]

    def process(d, tile):
        g = groups[d]
        wait_halo(d, tile)
        unpack(d, tile, g)
        filter_rows(g, local[0])
        for level in range(local_levels):
            last = level == local_levels - 1
            half = 2**level
            pairs = [j for j in range(ep_local) if not j & half]
            top = g * ep_local + ep_local - 2 * half
            level_pass(
                level, local[level], wide[0] if last else local[level + 1],
                g * ep_local, pairs, up_to(VMAX * top, STEP), g * ep_local if last else 0,
            )

    def finish(tile):
        for level in range(local_levels, LEVELS - 1):
            half = 2**level
            for first in range(0, epochs, 2 * half):
                level_pass(
                    level, wide[level - local_levels], wide[level - local_levels + 1], 0,
                    list(range(first, first + half)), up_to(VMAX * first, STEP), 0,
                )
        final = wide[LEVELS - 1 - local_levels]
        half = epochs // 2

        def body(b, carry):
            at = row_at(b, SUB)
            likelihood = [None] * epochs
            for j in range(half):
                lower = [final[j, m, pl.ds(at, SUB), :] for m in range(2)]
                for index in (j, j + half):
                    near, far, fraction = shift_of(LEVELS - 1, index)
                    maps = []
                    for m in range(2):
                        x = final[j + half, m, pl.ds(at - near, SUB), :]
                        y = final[j + half, m, pl.ds(at - far, SUB), :]
                        maps.append(lower[m] + ((1.0 - fraction) * x + fraction * y))
                    likelihood[index] = maps[0] * lax.rsqrt(maps[1])
            peak = functools.reduce(jnp.maximum, likelihood)
            total = functools.reduce(jnp.add, [jnp.exp(x - peak) for x in likelihood])
            to = pl.multiple_of(b * SUB, SUB)
            out[pl.ds(to, SUB), tile * LANES:(tile + 1) * LANES] = peak + jnp.log(total)
            return carry

        lax.fori_loop(0, blocks, body, 0)

    make_bands()
    for tile in range(tiles):
        for d in SEND_ORDER(n):
            filter_cols(groups[d], tile, outgoing.at[d - 1, tile] if d else pieces.at[0, tile])
            if tile == 0 and d == SEND_ORDER(n)[0]:
                near = jnp.where(has_above, 1, 0) + jnp.where(has_below, 1, 0)
                pl.semaphore_wait(barrier, n - 1 + near)
            if d:
                piece_copy(d, tile).start()
            else:
                forward(0, tile)

    for edge, part in ((has_above, 0), (has_below, 2)):
        @pl.when(jnp.logical_not(edge))
        def _():
            for ref in (rows_in,) + stacks:
                zero = jnp.zeros((row_count, LANES), jnp.float32)

                def body(e, carry):
                    for m in range(2):
                        ref[e, m, pl.ds(part * row_count, row_count), :] = zero
                    return carry

                lax.fori_loop(0, ref.shape[0], body, 0)

    steps = [(tile, d) for tile in range(tiles) for d in range(n)]
    for i in range(len(steps) + LAG):
        if i < len(steps):
            tile, d = steps[i]
            if d:
                piece_copy(d, tile).wait_recv()
                forward(d, tile)
        if i >= LAG:
            tile, d = steps[i - LAG]
            process(d, tile)
            if d == n - 1:
                finish(tile)

    for tile, d in steps:
        if d:
            piece_copy(d, tile).wait_send()
        wait_sent(d, tile)


def on_device(n, sky, image, inv_variance, psf_rows, psf_cols, shift_num):
    ep_local, row_count, cols = image.shape
    tiles = cols // n // LANES
    local_levels = ep_local.bit_length() - 1
    piece = (tiles, ep_local, 2, row_count, LANES)

    def tall(count):
        return pltpu.VMEM((count, 2, 3 * row_count, LANES), jnp.float32)

    vmem = pl.BlockSpec(memory_space=pltpu.VMEM)
    smem = pl.BlockSpec(memory_space=pltpu.SMEM)
    return pl.pallas_call(
        functools.partial(kernel, n, sky),
        out_shape=jax.ShapeDtypeStruct((row_count, cols // n), jnp.float32),
        in_specs=[vmem, vmem, smem, smem, smem],
        out_specs=vmem,
        scratch_shapes=[
            pltpu.VMEM((n - 1,) + piece, jnp.bfloat16),
            pltpu.VMEM((n,) + piece, jnp.bfloat16),
            pltpu.VMEM((n,) + piece, jnp.bfloat16),
            pltpu.VMEM((n,) + piece, jnp.bfloat16),
            pltpu.VMEM((2, 2 * LANES, 2 * LANES), jnp.bfloat16),
            tall(ep_local),
        ]
        + [tall(ep_local) for _ in range(local_levels)]
        + [tall(n * ep_local) for _ in range(LEVELS - local_levels)]
        + [pltpu.SemaphoreType.DMA((n, tiles)) for _ in range(6)],
        compiler_params=pltpu.CompilerParams(
            collective_id=0, has_side_effects=True, vmem_limit_bytes=60 * 1024 * 1024
        ),
    )(image, inv_variance, psf_rows, psf_cols, shift_num)


def solution(mesh):
    body = functools.partial(on_device, mesh.shape["epoch"], mesh.shape["sky"])
    return jax.shard_map(
        body,
        mesh=mesh,
        in_specs=(P("epoch", "sky", None), P("epoch", "sky", None), P(), P(), P()),
        out_specs=P("sky", "epoch"),
        check_vma=False,
    )
```
